32 devices in a mesh: row: 4 (over x, core), col: 8 (over z, y).
Axes of the slice: x: 2, y: 2, z: 4, core: 2. Of those that a mesh axis runs over, the one named last changes fastest.
Arguments:
- weight: bfloat16 [8192, 16384], P('row', 'col'), may hold values from -6 to 6
- gradient: bfloat16 [8192, 16384], P('row', 'col'), may hold values from -6 to 6
- old_basis: bfloat16 [8192, 1024], P('row'), may hold values from -0.0625 to 0.0625
- new_basis: bfloat16 [8192, 1024], P('row'), may hold values from -0.0625 to 0.0625
- first_moment: float32 [1024, 16384], P(None, ('col', 'row')), may hold values from -6 to 6
- second_moment: float32 [1024, 16384], P(None, ('col', 'row')), may hold values from 0.05 to 2
Outputs:
- new_weight: bfloat16 [8192, 16384], P('row', 'col')
- update: bfloat16 [8192, 16384], P('row', 'col')
- first_new: float32 [1024, 16384], P(None, ('col', 'row'))
- second_new: float32 [1024, 16384], P(None, ('col', 'row'))
The draws below stay inside these ranges and needn't reach their ends.
All inputs are finite; a program needn't handle non-finite values.
Results may differ from the reference program's by a relative error of at most 0.0047.
Values may be sent and summed in bfloat16 or wider, within the bound.
A program may use at most 128 MiB of HBM per device.

```python
import math
import jax
import jax.numpy as jnp
from jax import lax

D = 8192
FF = 16384
RANK = 1024


def levels(stream_key, dims, shards, low, largest):
    loudness, own = 1.0, jax.random.fold_in(stream_key, 6)
    for position, shards_of in shards:
        steps = jnp.exp(jax.random.uniform(jax.random.fold_in(own, position), (shards_of,), jnp.float32, low / len(shards), largest / len(shards)))
        loudness = loudness * jnp.repeat(steps, dims[position] // shards_of).reshape([-1 if axis == position else 1 for axis in range(len(dims))])
    return loudness


def gaussian(rng, extent, width, reach, pieces=(), held_as=jnp.bfloat16):
    values = width * jax.random.normal(rng, extent, jnp.float32)
    if pieces:
        values = values * levels(rng, extent, pieces, -0.22, 0.18)
    return jnp.clip(values, -reach, reach).astype(held_as)


def setup_inputs(seed: int = 0) -> dict:
    seeds = jax.random.split(jax.random.key(seed), 7)
    return {
        "weight": gaussian(seeds[0], (D, FF), 1.0, 6.0, ((0, 4), (1, 8))),
        "gradient": gaussian(seeds[1], (D, FF), 1.0, 6.0, ((0, 4), (1, 8))),
        "old_basis": gaussian(seeds[2], (D, RANK), D ** -0.5, 0.0625, ((0, 4),)),
        "new_basis": gaussian(seeds[3], (D, RANK), D ** -0.5, 0.0625, ((0, 4),)),
        "first_moment": gaussian(seeds[4], (RANK, FF), 1.0, 6.0, ((1, 32),), jnp.float32),
        "second_moment": jnp.clip(jnp.exp(math.log(2.0) - 3.6888794 * jax.random.uniform(seeds[5], (RANK, FF), jnp.float32) ** levels(seeds[5], (RANK, FF), ((1, 32),), -0.2, 0.2)), 0.05, 2.0),
    }


beta_first = 0.9
beta_second = 0.95
epsilon = 1e-08
step_rate = 0.0025

def reference(weight, gradient, old_basis, new_basis, first_moment, second_moment):
    transition = jnp.dot(new_basis.T, old_basis, preferred_element_type=jnp.float32)
    projected = jnp.dot(new_basis.T, gradient, preferred_element_type=jnp.float32)
    moved_first = jnp.dot(transition, first_moment, precision=lax.Precision.HIGHEST)
    moved_second = jnp.dot(transition * transition, second_moment, precision=lax.Precision.HIGHEST)
    first_new = beta_first * moved_first + (1.0 - beta_first) * projected
    second_new = beta_second * moved_second + (1.0 - beta_second) * projected * projected
    direction = (first_new / (jnp.sqrt(second_new) + epsilon)).astype(jnp.bfloat16)
    back = jnp.dot(new_basis, direction, preferred_element_type=jnp.float32)
    new_weight = (weight.astype(jnp.float32) - step_rate * back).astype(jnp.bfloat16)
    return (new_weight, back.astype(jnp.bfloat16), first_new, second_new)
```

```python
import jax
import jax.numpy as jnp
from jax import lax
from jax.sharding import PartitionSpec as P

beta_first = 0.9
beta_second = 0.95
epsilon = 1e-08
step_rate = 0.0025


def shards(columns, weight, gradient, old_basis, new_basis, first_moment, second_moment):
    part = old_basis.shape[1] // columns
    mine = lax.dynamic_slice_in_dim(old_basis, lax.axis_index("col") * part, part, axis=1)
    partial_sums = jnp.einsum("mr,mn->rn", new_basis, gradient, preferred_element_type=jnp.float32)
    projected = lax.psum_scatter(partial_sums.astype(jnp.bfloat16), "row", scatter_dimension=1, tiled=True)
    local_term = jnp.einsum("mc,mr->cr", mine, new_basis, preferred_element_type=jnp.float32)
    flipped = lax.all_gather(lax.psum(local_term, "row").astype(jnp.bfloat16), "col", axis=0, tiled=True)
    squares = jnp.square(flipped.astype(jnp.float32)).astype(jnp.bfloat16)
    moved_first = jnp.einsum("cr,cn->rn", flipped, first_moment.astype(jnp.bfloat16), preferred_element_type=jnp.float32)
    moved_second = jnp.einsum("cr,cn->rn", squares, second_moment.astype(jnp.bfloat16), preferred_element_type=jnp.float32)
    projected = projected.astype(jnp.float32)
    first_new = beta_first * moved_first + (1.0 - beta_first) * projected
    second_new = beta_second * moved_second + (1.0 - beta_second) * projected * projected
    direction = (first_new / (jnp.sqrt(second_new) + epsilon)).astype(jnp.bfloat16)
    back = jnp.dot(
        new_basis,
        lax.all_gather(direction, "row", axis=1, tiled=True),
        preferred_element_type=jnp.float32,
    )
    new_weight = (weight.astype(jnp.float32) - step_rate * back).astype(jnp.bfloat16)
    return (new_weight, back.astype(jnp.bfloat16), first_new, second_new)


def solution(mesh):
    placed = (
        P("row", "col"),
        P("row", "col"),
        P("row", None),
        P("row", None),
        P(None, ("col", "row")),
        P(None, ("col", "row")),
    )
    return jax.shard_map(
        lambda *blocks: shards(mesh.shape["col"], *blocks),
        mesh=mesh,
        in_specs=placed,
        out_specs=(
            P("row", "col"),
            P("row", "col"),
            P(None, ("col", "row")),
            P(None, ("col", "row")),
        ),
        check_vma=False,
    )
```

```python
import jax
import jax.numpy as jnp
from jax import lax
from jax.sharding import PartitionSpec as P

beta_first = 0.9
beta_second = 0.95
epsilon = 1e-08
step_rate = 0.0025


def low(values):
    return values.astype(jnp.bfloat16)


def wide(values):
    return values.astype(jnp.float32)


def product(left, right):
    return jnp.einsum("mr,mn->rn", left, right, preferred_element_type=jnp.float32)


def transposed_transition(columns, old_basis, new_basis):
    part = old_basis.shape[1] // columns
    mine = lax.dynamic_slice_in_dim(old_basis, lax.axis_index("col") * part, part, axis=1)
    summed = lax.psum(product(mine, new_basis), "row")
    return lax.all_gather(low(summed), "col", axis=0, tiled=True)


def swaps(rows):
    core = [(r, r ^ 1) for r in range(rows)]
    chip = [(r, r ^ 2) for r in range(rows)]
    return core, chip


def shards(rows, columns, weight, gradient, old_basis, new_basis, first_moment, second_moment):
    flipped = transposed_transition(columns, old_basis, new_basis)
    squares = low(jnp.square(wide(flipped)))
    moved_first = product(flipped, low(first_moment))
    moved_second = product(squares, low(second_moment))
    width = first_moment.shape[1]
    row = lax.axis_index("row")
    here, core_mate, chip_mate, diagonal = (row ^ k for k in range(4)) if rows == 4 else (row,) * 4
    if rows == 4:
        core, chip = swaps(rows)

        def partial(block):
            piece = lax.dynamic_slice_in_dim(gradient, block * width, width, axis=1)
            return product(new_basis, piece)

        to_core_far = lax.ppermute(low(partial(diagonal)), "row", core)
        far = low(partial(chip_mate) + wide(to_core_far))
        from_chip = lax.ppermute(far, "row", chip)
        from_core = lax.ppermute(low(partial(core_mate)), "row", core)
        projected = partial(here) + wide(from_core) + wide(from_chip)
    else:
        sums = low(product(new_basis, gradient))
        projected = wide(lax.psum_scatter(sums, "row", scatter_dimension=1, tiled=True))
    first_new = beta_first * moved_first + (1.0 - beta_first) * projected
    second_new = beta_second * moved_second + (1.0 - beta_second) * projected * projected
    direction = low(first_new / (jnp.sqrt(second_new) + epsilon))
    if rows == 4:
        across = lax.ppermute(direction, "row", chip)
        beside = lax.ppermute(direction, "row", core)
        beyond = lax.ppermute(across, "row", core)
        directions = jnp.zeros((direction.shape[0], width * rows), direction.dtype)
        for block, values in ((here, direction), (core_mate, beside), (chip_mate, across), (diagonal, beyond)):
            directions = lax.dynamic_update_slice_in_dim(directions, values, block * width, axis=1)
    else:
        directions = lax.all_gather(direction, "row", axis=1, tiled=True)
    back = jnp.dot(new_basis, directions, preferred_element_type=jnp.float32)
    new_weight = low(wide(weight) - step_rate * back)
    return (new_weight, low(back), first_new, second_new)


def solution(mesh):
    placed = (
        P("row", "col"),
        P("row", "col"),
        P("row", None),
        P("row", None),
        P(None, ("col", "row")),
        P(None, ("col", "row")),
    )
    return jax.shard_map(
        lambda *blocks: shards(mesh.shape["row"], mesh.shape["col"], *blocks),
        mesh=mesh,
        in_specs=placed,
        out_specs=(
            P("row", "col"),
            P("row", "col"),
            P(None, ("col", "row")),
            P(None, ("col", "row")),
        ),
        check_vma=False,
    )
```

```python
import functools

import jax
import jax.numpy as jnp
from jax import lax
from jax.experimental import pallas as pl
from jax.experimental.pallas import tpu as pltpu
from jax.sharding import PartitionSpec as P

beta_first = 0.9
beta_second = 0.95
epsilon = 1e-08
step_rate = 0.0025

CHUNKS = 2


def low(values):
    return values.astype(jnp.bfloat16)


def wide(values):
    return values.astype(jnp.float32)


def product(left, right):
    return jnp.einsum("mr,mn->rn", left, right, preferred_element_type=jnp.float32)


def swap(values, axis, size, bit):
    return lax.ppermute(values, axis, [(k, k ^ bit) for k in range(size)])


def in_order(own, other, second, axis):
    return jnp.where(second == 1, jnp.stack([other, own], axis), jnp.stack([own, other], axis))


def paired_transition(rows, columns, old_basis, new_basis):
    part = old_basis.shape[1] // columns
    row, column = lax.axis_index("row"), lax.axis_index("col")
    core_at, layer = row & 1, column // 2
    layers = columns // 2
    mine = lax.dynamic_slice_in_dim(old_basis, column * part, part, axis=1)
    term = product(mine, new_basis)
    half = part // 2
    kept = lax.dynamic_slice_in_dim(term, core_at * half, half, axis=0)
    sent = lax.dynamic_slice_in_dim(term, (1 - core_at) * half, half, axis=0)
    kept = kept + wide(swap(low(sent), "row", rows, 1))
    piece = low(kept + wide(swap(low(kept), "row", rows, 2)))
    stack = [piece]
    for hop in range(1, layers):
        stack.append(lax.ppermute(piece, "col", [(k, (k + 2 * hop) % columns) for k in range(columns)]))
    stack = jnp.stack(stack[::-1] * 2)
    along = lax.dynamic_slice_in_dim(stack, layers - 1 - layer, layers, axis=0)
    both = in_order(along, swap(along, "col", columns, 1), column & 1, 1)
    whole = in_order(both, swap(both, "row", rows, 1), core_at, 2)
    return whole.reshape(old_basis.shape[1], new_basis.shape[1])


def plain_transition(columns, old_basis, new_basis):
    part = old_basis.shape[1] // columns
    mine = lax.dynamic_slice_in_dim(old_basis, lax.axis_index("col") * part, part, axis=1)
    summed = lax.psum(product(mine, new_basis), "row")
    return lax.all_gather(low(summed), "col", axis=0, tiled=True)


def stepped(flipped, squares, first_moment, second_moment, projected):
    moved_first = product(flipped, first_moment)
    moved_second = product(squares, second_moment)
    first_new = beta_first * moved_first + (1.0 - beta_first) * projected
    second_new = beta_second * moved_second + (1.0 - beta_second) * projected * projected
    return first_new, second_new, low(first_new / (jnp.sqrt(second_new) + epsilon))


def back_kernel(width, chunks, place, basis, weight, *rest):
    directions, (new_weight, update) = rest[: 2 * chunks], rest[-2:]
    ranks = basis.shape[1] // chunks

    def put(pieces, columns):
        back = jnp.zeros((basis.shape[0], width), jnp.float32)
        for k, piece in enumerate(pieces):
            back += jnp.dot(
                basis[:, k * ranks : (k + 1) * ranks], piece[...], preferred_element_type=jnp.float32
            )
        update[:, columns] = low(back)
        new_weight[:, columns] = low(wide(weight[:, columns]) - step_rate * back)

    for core in range(2):

        @pl.when(place[1] == core)
        def _():
            put(directions[:chunks], slice(core * width, (core + 1) * width))
            put(directions[chunks:], slice((1 - core) * width, (2 - core) * width))


def back_half(place, basis, weight, mine, mate, held=()):
    depth, ranks = basis.shape
    width = mine[0].shape[1]
    tile = min(512, depth)
    whole = pl.BlockSpec(mine[0].shape, lambda i, place: (0, 0))
    block = pl.BlockSpec((tile, 2 * width), lambda i, place: (i, place[0]))
    directions = [*mine, *mate]
    return pl.pallas_call(
        functools.partial(back_kernel, width, len(mine)),
        out_shape=[jax.ShapeDtypeStruct(weight.shape, jnp.bfloat16)] * 2,
        grid_spec=pltpu.PrefetchScalarGridSpec(
            num_scalar_prefetch=1,
            grid=(depth // tile,),
            in_specs=[pl.BlockSpec((tile, ranks), lambda i, place: (i, 0)), block]
            + [whole] * len(directions)
            + [pl.BlockSpec(memory_space=pl.ANY)] * len(held),
            out_specs=[block] * 2,
        ),
        input_output_aliases={3 + len(directions) + k: k for k in range(len(held))},
        compiler_params=pltpu.CompilerParams(vmem_limit_bytes=32 << 20),
        cost_estimate=pl.CostEstimate(
            flops=4 * depth * ranks * width,
            bytes_accessed=2 * (depth * ranks + 6 * depth * width + 2 * ranks * width),
            transcendentals=0,
        ),
    )(place, basis, weight, *directions, *held)


def paired(rows, columns, weight, gradient, old_basis, new_basis, first_moment, second_moment):
    width = first_moment.shape[1]
    row = lax.axis_index("row")
    chip_at, core_at = row >> 1, row & 1
    chunk = new_basis.shape[1] // CHUNKS
    parts = [slice(k * chunk, (k + 1) * chunk) for k in range(CHUNKS)]

    def columns_of(chip, after=None):
        source = gradient if after is None else lax.optimization_barrier((gradient, after))[0]
        return lax.dynamic_slice_in_dim(source, chip * 2 * width, 2 * width, axis=1)

    def block(values, core):
        return lax.dynamic_slice_in_dim(values, core * width, width, axis=1)

    far = [product(new_basis[:, part], columns_of(1 - chip_at)) for part in parts]
    far_mate = [swap(low(block(values, 1 - core_at)), "row", rows, 1) for values in far]
    far = [low(block(values, core_at) + wide(mate)) for values, mate in zip(far, far_mate)]
    from_chip = [swap(values, "row", rows, 2) for values in far]
    near = [product(new_basis[:, part], columns_of(chip_at, sent)) for part, sent in zip(parts, far)]
    from_core = [swap(low(block(values, 1 - core_at)), "row", rows, 1) for values in near]
    flipped = paired_transition(rows, columns, old_basis, new_basis)
    squares = low(jnp.square(wide(flipped)))
    first_moment, second_moment = low(first_moment), low(second_moment)
    steps = [
        stepped(
            flipped[:, part],
            squares[:, part],
            first_moment,
            second_moment,
            block(near[k], core_at) + wide(from_core[k]) + wide(from_chip[k]),
        )
        for k, part in enumerate(parts)
    ]
    direction = [step[2] for step in steps]
    across = [swap(values, "row", rows, 2) for values in direction]
    beside = [swap(values, "row", rows, 1) for values in direction]
    beyond = [swap(values, "row", rows, 1) for values in across]
    held = back_half(jnp.stack([chip_at, core_at]), new_basis, weight, direction, beside)
    new_weight, update = back_half(jnp.stack([1 - chip_at, core_at]), new_basis, weight, across, beyond, held)
    return (new_weight, update, *(jnp.concatenate([step[k] for step in steps]) for k in range(2)))


def plain(columns, weight, gradient, old_basis, new_basis, first_moment, second_moment):
    flipped = plain_transition(columns, old_basis, new_basis)
    squares = low(jnp.square(wide(flipped)))
    sums = low(product(new_basis, gradient))
    projected = wide(lax.psum_scatter(sums, "row", scatter_dimension=1, tiled=True))
    first_new, second_new, direction = stepped(
        flipped, squares, low(first_moment), low(second_moment), projected
    )
    directions = lax.all_gather(direction, "row", axis=1, tiled=True)
    back = jnp.dot(new_basis, directions, preferred_element_type=jnp.float32)
    new_weight = low(wide(weight) - step_rate * back)
    return (new_weight, low(back), first_new, second_new)


def solution(mesh):
    rows, columns = mesh.shape["row"], mesh.shape["col"]
    pairs = rows == 4 and columns % 2 == 0
    placed = (
        P("row", "col"),
        P("row", "col"),
        P("row", None),
        P("row", None),
        P(None, ("col", "row")),
        P(None, ("col", "row")),
    )
    return jax.shard_map(
        functools.partial(paired, rows, columns) if pairs else functools.partial(plain, columns),
        mesh=mesh,
        in_specs=placed,
        out_specs=(
            P("row", "col"),
            P("row", "col"),
            P(None, ("col", "row")),
            P(None, ("col", "row")),
        ),
        check_vma=False,
    )
```

```python
import functools

import jax
import jax.numpy as jnp
from jax import lax
from jax.experimental import pallas as pl
from jax.experimental.pallas import tpu as pltpu
from jax.sharding import PartitionSpec as P


beta_first = 0.9
beta_second = 0.95
epsilon = 1e-08
step_rate = 0.0025

CHUNKS = 2


def low(values):
    return values.astype(jnp.bfloat16)


def wide(values):
    return values.astype(jnp.float32)


def product(left, right):
    return jnp.einsum("mr,mn->rn", left, right, preferred_element_type=jnp.float32)


def swap(values, axis, size, bit):
    return lax.ppermute(values, axis, [(k, k ^ bit) for k in range(size)])


def after(values, *earlier):
    return lax.optimization_barrier((values, earlier))[0]


def in_order(own, other, second, axis):
    return jnp.where(second == 1, jnp.stack([other, own], axis), jnp.stack([own, other], axis))


def transition_piece(rows, columns, old_basis, new_basis):
    part = old_basis.shape[1] // columns
    core_at = lax.axis_index("row") & 1
    mine = lax.dynamic_slice_in_dim(old_basis, lax.axis_index("col") * part, part, axis=1)
    term = product(mine, new_basis)
    half = part // 2
    kept = lax.dynamic_slice_in_dim(term, core_at * half, half, axis=0)
    sent = lax.dynamic_slice_in_dim(term, (1 - core_at) * half, half, axis=0)
    kept = kept + swap(sent, "row", rows, 1)
    return low(kept + wide(swap(low(kept), "row", rows, 2))), kept


def along_layers(piece, columns):
    received = []
    for hop in range(1, columns // 2):
        received.append(lax.ppermute(piece, "col", [(k, (k + 2 * hop) % columns) for k in range(columns)]))
    return received


def layers_in_order(piece, received):
    layers = 1 + len(received)
    stack = jnp.concatenate([piece, *received][::-1] * 2)
    first = (layers - 1 - lax.axis_index("col") // 2) * piece.shape[0]
    return lax.dynamic_slice_in_dim(stack, first, layers * piece.shape[0], axis=0).reshape(layers, *piece.shape)


def plain_transition(columns, old_basis, new_basis):
    part = old_basis.shape[1] // columns
    mine = lax.dynamic_slice_in_dim(old_basis, lax.axis_index("col") * part, part, axis=1)
    summed = lax.psum(product(mine, new_basis), "row")
    return lax.all_gather(low(summed), "col", axis=0, tiled=True)


def stepped(flipped, squares, first_moment, second_moment, projected):
    moved_first = product(flipped, first_moment)
    moved_second = product(squares, second_moment)
    first_new = beta_first * moved_first + (1.0 - beta_first) * projected
    second_new = beta_second * moved_second + (1.0 - beta_second) * projected * projected
    return first_new, second_new, low(first_new / (jnp.sqrt(second_new) + epsilon))


def back_kernel(width, chunks, place, basis, weight, *rest):
    directions, (new_weight, update) = rest[: 2 * chunks], rest[-2:]
    ranks = basis.shape[1] // chunks

    def put(pieces, columns):
        back = jnp.zeros((basis.shape[0], width), jnp.float32)
        for k, piece in enumerate(pieces):
            back += jnp.dot(
                basis[:, k * ranks : (k + 1) * ranks], piece[...], preferred_element_type=jnp.float32
            )
        update[:, columns] = low(back)
        new_weight[:, columns] = low(wide(weight[:, columns]) - step_rate * back)

    for core in range(2):

        @pl.when(place[1] == core)
        def _():
            put(directions[:chunks], slice(core * width, (core + 1) * width))
            put(directions[chunks:], slice((1 - core) * width, (2 - core) * width))


def back_half(place, basis, weight, mine, mate, held=()):
    depth, ranks = basis.shape
    width = mine[0].shape[1]
    tile = min(512, depth)
    whole = pl.BlockSpec(mine[0].shape, lambda i, place: (0, 0))
    block = pl.BlockSpec((tile, 2 * width), lambda i, place: (i, place[0]))
    directions = [*mine, *mate]
    return pl.pallas_call(
        functools.partial(back_kernel, width, len(mine)),
        out_shape=[jax.ShapeDtypeStruct(weight.shape, jnp.bfloat16)] * 2,
        grid_spec=pltpu.PrefetchScalarGridSpec(
            num_scalar_prefetch=1,
            grid=(depth // tile,),
            in_specs=[pl.BlockSpec((tile, ranks), lambda i, place: (i, 0)), block]
            + [whole] * len(directions)
            + [pl.BlockSpec(memory_space=pl.ANY)] * len(held),
            out_specs=[block] * 2,
        ),
        input_output_aliases={3 + len(directions) + k: k for k in range(len(held))},
        compiler_params=pltpu.CompilerParams(vmem_limit_bytes=32 << 20),
        cost_estimate=pl.CostEstimate(
            flops=4 * depth * ranks * width,
            bytes_accessed=2 * (depth * ranks + 6 * depth * width + 2 * ranks * width),
            transcendentals=0,
        ),
    )(place, basis, weight, *directions, *held)


def paired(rows, columns, weight, gradient, old_basis, new_basis, first_moment, second_moment):
    width = first_moment.shape[1]
    row = lax.axis_index("row")
    chip_at, core_at = row >> 1, row & 1
    chunk = new_basis.shape[1] // CHUNKS
    parts = [slice(k * chunk, (k + 1) * chunk) for k in range(CHUNKS)]

    def columns_of(source, chip):
        return lax.dynamic_slice_in_dim(source, chip * 2 * width, 2 * width, axis=1)

    def block(values, core):
        return lax.dynamic_slice_in_dim(values, core * width, width, axis=1)

    piece, earlier = transition_piece(rows, columns, old_basis, new_basis)
    received = along_layers(piece, columns)
    far, source = [], after(gradient, earlier)
    for part in parts:
        values = product(new_basis[:, part], columns_of(source, 1 - chip_at))
        mate = swap(low(block(values, 1 - core_at)), "row", rows, 1)
        far.append(low(block(values, core_at) + wide(mate)))
        source = after(gradient, far[-1])
    from_chip = []
    for values in far:
        from_chip.append(swap(values, "row", rows, 2))
    near, from_core = [], []
    for k, part in enumerate(parts):
        values = product(new_basis[:, part], columns_of(source, chip_at))
        near.append(block(values, core_at))
        mate = low(block(values, 1 - core_at))
        from_core.append(swap(mate, "row", rows, 1))
        if k == 0:
            along = layers_in_order(piece, after(received, mate))
            beyond = swap(along, "col", columns, 1)
            source = after(gradient, along)
    both = in_order(along, after(beyond, mate), lax.axis_index("col") & 1, 1)
    flipped = in_order(both, swap(both, "row", rows, 1), core_at, 2)
    flipped = flipped.reshape(old_basis.shape[1], new_basis.shape[1])
    squares = low(jnp.square(wide(flipped)))
    first_moment, second_moment = low(first_moment), low(second_moment)
    steps, across = [], []
    for k, part in enumerate(parts):
        projected = near[k] + wide(from_core[k]) + wide(from_chip[k])
        steps.append(stepped(flipped[:, part], squares[:, part], first_moment, second_moment, projected))
        across.append(swap(steps[k][2], "row", rows, 2))
    direction = [step[2] for step in steps]
    beside = [swap(values, "row", rows, 1) for values in direction]
    held = back_half(jnp.stack([chip_at, core_at]), new_basis, weight, direction, beside)
    first_new, second_new = (jnp.concatenate([step[k] for step in steps]) for k in range(2))
    across = after(across, held, first_new, second_new)
    beyond = [swap(values, "row", rows, 1) for values in across]
    new_weight, update = back_half(jnp.stack([1 - chip_at, core_at]), new_basis, weight, across, beyond, held)
    return (new_weight, update, first_new, second_new)


def plain(columns, weight, gradient, old_basis, new_basis, first_moment, second_moment):
    flipped = plain_transition(columns, old_basis, new_basis)
    squares = low(jnp.square(wide(flipped)))
    sums = low(product(new_basis, gradient))
    projected = wide(lax.psum_scatter(sums, "row", scatter_dimension=1, tiled=True))
    first_new, second_new, direction = stepped(
        flipped, squares, low(first_moment), low(second_moment), projected
    )
    directions = lax.all_gather(direction, "row", axis=1, tiled=True)
    back = jnp.dot(new_basis, directions, preferred_element_type=jnp.float32)
    new_weight = low(wide(weight) - step_rate * back)
    return (new_weight, low(back), first_new, second_new)


def solution(mesh):
    rows, columns = mesh.shape["row"], mesh.shape["col"]
    pairs = rows == 4 and columns % 2 == 0
    placed = (
        P("row", "col"),
        P("row", "col"),
        P("row", None),
        P("row", None),
        P(None, ("col", "row")),
        P(None, ("col", "row")),
    )
    return jax.shard_map(
        functools.partial(paired, rows, columns) if pairs else functools.partial(plain, columns),
        mesh=mesh,
        in_specs=placed,
        out_specs=(
            P("row", "col"),
            P("row", "col"),
            P(None, ("col", "row")),
            P(None, ("col", "row")),
        ),
        check_vma=False,
    )
```

```python
import functools

import jax
import jax.numpy as jnp
from jax import lax
from jax.experimental import pallas as pl
from jax.experimental.pallas import tpu as pltpu
from jax.sharding import PartitionSpec as P


beta_first = 0.9
beta_second = 0.95
epsilon = 1e-08
step_rate = 0.0025

CHUNKS = 2


def low(values):
    return values.astype(jnp.bfloat16)


def wide(values):
    return values.astype(jnp.float32)


def product(left, right):
    return jnp.einsum("mr,mn->rn", left, right, preferred_element_type=jnp.float32)


def swap(values, axis, size, bit):
    return lax.ppermute(values, axis, [(k, k ^ bit) for k in range(size)])


def after(values, *earlier):
    return lax.optimization_barrier((values, earlier))[0]


def in_order(own, other, second, axis):
    return jnp.where(second == 1, jnp.stack([other, own], axis), jnp.stack([own, other], axis))


def transition_piece(rows, columns, old_basis, new_basis):
    part = old_basis.shape[1] // columns
    core_at = lax.axis_index("row") & 1
    mine = lax.dynamic_slice_in_dim(old_basis, lax.axis_index("col") * part, part, axis=1)
    term = product(mine, new_basis)
    half = part // 2
    kept = lax.dynamic_slice_in_dim(term, core_at * half, half, axis=0)
    sent = lax.dynamic_slice_in_dim(term, (1 - core_at) * half, half, axis=0)
    kept = kept + swap(sent, "row", rows, 1)
    return low(kept + wide(swap(low(kept), "row", rows, 2))), kept


def along_layers(piece, columns):
    received = []
    for hop in range(1, columns // 2):
        received.append(lax.ppermute(piece, "col", [(k, (k + 2 * hop) % columns) for k in range(columns)]))
    return received


def layers_in_order(piece, received):
    layers = 1 + len(received)
    stack = jnp.concatenate([piece, *received][::-1] * 2)
    first = (layers - 1 - lax.axis_index("col") // 2) * piece.shape[0]
    return lax.dynamic_slice_in_dim(stack, first, layers * piece.shape[0], axis=0).reshape(layers, *piece.shape)


def plain_transition(columns, old_basis, new_basis):
    part = old_basis.shape[1] // columns
    mine = lax.dynamic_slice_in_dim(old_basis, lax.axis_index("col") * part, part, axis=1)
    summed = lax.psum(product(mine, new_basis), "row")
    return lax.all_gather(low(summed), "col", axis=0, tiled=True)


def stepped(flipped, squares, first_moment, second_moment, projected):
    moved_first = product(flipped, first_moment)
    moved_second = product(squares, second_moment)
    first_new = beta_first * moved_first + (1.0 - beta_first) * projected
    second_new = beta_second * moved_second + (1.0 - beta_second) * projected * projected
    return first_new, second_new, low(first_new / (jnp.sqrt(second_new) + epsilon))


def back_kernel(width, chunks, place, basis, weight, *rest):
    directions, (new_weight, update) = rest[: 2 * chunks], rest[-2:]
    ranks = basis.shape[1] // chunks

    def put(pieces, columns):
        back = jnp.zeros((basis.shape[0], width), jnp.float32)
        for k, piece in enumerate(pieces):
            back += jnp.dot(
                basis[:, k * ranks : (k + 1) * ranks], piece[...], preferred_element_type=jnp.float32
            )
        update[:, columns] = low(back)
        new_weight[:, columns] = low(wide(weight[:, columns]) - step_rate * back)

    for core in range(2):

        @pl.when(place[1] == core)
        def _():
            put(directions[:chunks], slice(core * width, (core + 1) * width))
            put(directions[chunks:], slice((1 - core) * width, (2 - core) * width))


def back_half(place, basis, weight, mine, mate, held=()):
    depth, ranks = basis.shape
    width = mine[0].shape[1]
    tile = min(512, depth)
    whole = pl.BlockSpec(mine[0].shape, lambda i, place: (0, 0))
    block = pl.BlockSpec((tile, 2 * width), lambda i, place: (i, place[0]))
    directions = [*mine, *mate]
    return pl.pallas_call(
        functools.partial(back_kernel, width, len(mine)),
        out_shape=[jax.ShapeDtypeStruct(weight.shape, jnp.bfloat16)] * 2,
        grid_spec=pltpu.PrefetchScalarGridSpec(
            num_scalar_prefetch=1,
            grid=(depth // tile,),
            in_specs=[pl.BlockSpec((tile, ranks), lambda i, place: (i, 0)), block]
            + [whole] * len(directions)
            + [pl.BlockSpec(memory_space=pl.ANY)] * len(held),
            out_specs=[block] * 2,
        ),
        input_output_aliases={3 + len(directions) + k: k for k in range(len(held))},
        compiler_params=pltpu.CompilerParams(vmem_limit_bytes=32 << 20),
        cost_estimate=pl.CostEstimate(
            flops=4 * depth * ranks * width,
            bytes_accessed=2 * (depth * ranks + 6 * depth * width + 2 * ranks * width),
            transcendentals=0,
        ),
    )(place, basis, weight, *directions, *held)


def paired(rows, columns, weight, gradient, old_basis, new_basis, first_moment, second_moment):
    width = first_moment.shape[1]
    row = lax.axis_index("row")
    chip_at, core_at = row >> 1, row & 1
    chunk = new_basis.shape[1] // CHUNKS
    parts = [slice(k * chunk, (k + 1) * chunk) for k in range(CHUNKS)]

    def columns_of(source, chip):
        return lax.dynamic_slice_in_dim(source, chip * 2 * width, 2 * width, axis=1)

    def block(values, core):
        return lax.dynamic_slice_in_dim(values, core * width, width, axis=1)

    piece, earlier = transition_piece(rows, columns, old_basis, new_basis)
    received = along_layers(piece, columns)
    far, source = [], after(gradient, earlier)
    for part in parts:
        values = product(new_basis[:, part], columns_of(source, 1 - chip_at))
        mate = swap(low(block(values, 1 - core_at)), "row", rows, 1)
        far.append(low(block(values, core_at) + wide(mate)))
        source = after(gradient, far[-1])
    from_chip = []
    for values in far:
        from_chip.append(swap(values, "row", rows, 2))
    near, from_core = [], []
    for k, part in enumerate(parts):
        values = product(new_basis[:, part], columns_of(source, chip_at))
        near.append(block(values, core_at))
        mate = low(block(values, 1 - core_at))
        from_core.append(swap(mate, "row", rows, 1))
        if k == 0:
            along = layers_in_order(piece, after(received, mate))
            along = [along[:, :, each] for each in parts]
            beyond = []
            for values in along:
                beyond.append(swap(values, "col", columns, 1))
            source = after(gradient, along)
    first_moment, second_moment = low(first_moment), low(second_moment)
    steps, across = [], []
    earlier = mate
    for k in range(CHUNKS):
        both = in_order(along[k], after(beyond[k], earlier), lax.axis_index("col") & 1, 1)
        flipped = in_order(both, swap(both, "row", rows, 1), core_at, 2).reshape(-1, chunk)
        squares = low(jnp.square(wide(flipped)))
        projected = near[k] + wide(from_core[k]) + wide(from_chip[k])
        steps.append(stepped(flipped, squares, first_moment, second_moment, projected))
        earlier = steps[k][2]
        across.append(swap(steps[k][2], "row", rows, 2))
    direction = [step[2] for step in steps]
    beside = [swap(values, "row", rows, 1) for values in direction]
    held = back_half(jnp.stack([chip_at, core_at]), new_basis, weight, direction, beside)
    first_new, second_new = (jnp.concatenate([step[k] for step in steps]) for k in range(2))
    across = after(across, held, first_new, second_new)
    beyond = [swap(values, "row", rows, 1) for values in across]
    new_weight, update = back_half(jnp.stack([1 - chip_at, core_at]), new_basis, weight, across, beyond, held)
    return (new_weight, update, first_new, second_new)


def plain(columns, weight, gradient, old_basis, new_basis, first_moment, second_moment):
    flipped = plain_transition(columns, old_basis, new_basis)
    squares = low(jnp.square(wide(flipped)))
    sums = low(product(new_basis, gradient))
    projected = wide(lax.psum_scatter(sums, "row", scatter_dimension=1, tiled=True))
    first_new, second_new, direction = stepped(
        flipped, squares, low(first_moment), low(second_moment), projected
    )
    directions = lax.all_gather(direction, "row", axis=1, tiled=True)
    back = jnp.dot(new_basis, directions, preferred_element_type=jnp.float32)
    new_weight = low(wide(weight) - step_rate * back)
    return (new_weight, low(back), first_new, second_new)


def solution(mesh):
    rows, columns = mesh.shape["row"], mesh.shape["col"]
    pairs = rows == 4 and columns % 2 == 0
    placed = (
        P("row", "col"),
        P("row", "col"),
        P("row", None),
        P("row", None),
        P(None, ("col", "row")),
        P(None, ("col", "row")),
    )
    return jax.shard_map(
        functools.partial(paired, rows, columns) if pairs else functools.partial(plain, columns),
        mesh=mesh,
        in_specs=placed,
        out_specs=(
            P("row", "col"),
            P("row", "col"),
            P(None, ("col", "row")),
            P(None, ("col", "row")),
        ),
        check_vma=False,
    )
```
